32 devices in a mesh: grp: 8 (over z, core), dev: 4 (over y, x).
Axes of the slice: x: 2, y: 2, z: 4, core: 2. Of those that a mesh axis runs over, the one named last changes fastest.
Arguments:
- orbitals: bfloat16 [64, 256, 1024], P(('grp', 'dev')), may hold values from -6 to 6
- dens_tiles: bfloat16 [1024, 128, 128], P(('grp', 'dev')), may hold values from -0.005859375 to 0.005859375
- point_coords: float32 [3, 16384], P(None, ('grp', 'dev')), may hold values from 0 to 64
- point_weights: float32 [16384], P(('grp', 'dev')), may hold values from 0.005 to 0.05
- batch_blocks: int32 [64, 8], P(('grp', 'dev')), may hold values from 0 to 8, all different within a row
- tile_owner: int32 [2592, 1], P(('grp', 'dev')), may hold values from 0 to 3; in each aligned block of 81 rows (0 to 80, 81 to 161, ...) at most 31 rows name the same one
- tile_slot: int32 [2592], P(('grp', 'dev')), may hold values from 0 to 31
- batch_atoms: int32 [64, 4], P(('grp', 'dev')), may hold values from 0 to 3, all different within a row
- batch_weights: int32 [64, 4], P(('grp', 'dev')), may hold values from 1 to 8
- atom_grid_index: int32 [3, 32], P(None, 'grp'), may hold values from 0 to 63
Outputs:
- density: float32 [16384], P(('grp', 'dev'))
- potential: float32 [16384], P(('grp', 'dev'))
- ham_tiles: bfloat16 [1024, 128, 128], P(('grp', 'dev'))
The draws below stay inside these ranges and needn't reach their ends.
Inputs may be any that keep to these rules, and one draw needn't show every extreme that they name: `tile_owner`: in each aligned block of 81 rows (the listed tiles of one device) no owner is named by more than 31 rows, a bound that some block reaches. `batch_blocks`: the 8 blocks of a batch are distinct. `batch_atoms`: the 4 atoms of a batch are distinct.
All inputs are finite; a program needn't handle non-finite values.
Results may differ from the reference program's by a relative error of at most 0.0056.
Values may be sent and summed in bfloat16 or wider, within the bound.
A program may use at most 64 MiB of HBM per device.

```python
import math
import jax
import jax.numpy as jnp
import numpy as np
from jax import lax

TB = 128
BB = 8
BORB = 1024
UB = 9
R = 81
PTS = 256
BAT_DEV = 2
KM = 512
NEAR = 4
TILE_DEV = 32
GRIDN = 64
OWNERS = 4
CAP = 31
ATOM_GRP = 4
ATOMS = 32
BATCHES = 64
POINTS = 16384
TILES = 1024
REQS = 2592
N_GRP = 8
N_DEV = 4


def with_ends(array, key, smallest, largest):
    longest = array.shape.index(max(array.shape))
    spots = []
    for shift in (0, 1):
        where = [jax.random.randint(jax.random.fold_in(key, axis), (), 0, length) for axis, length in enumerate(array.shape)]
        where[longest] = (where[longest] + shift) % array.shape[longest]
        spots.append(tuple(where))
    return array.at[spots[0]].set(smallest).at[spots[1]].set(largest)


def level_of(key, dims, split, smallest, high):
    gain, own = 1.0, jax.random.fold_in(key, 6)
    for axis_at, shards_of in split:
        draws = jnp.exp(jax.random.uniform(jax.random.fold_in(own, axis_at), (shards_of,), jnp.float32, smallest / len(split), high / len(split)))
        gain = gain * jnp.repeat(draws, dims[axis_at] // shards_of).reshape([-1 if axis == axis_at else 1 for axis in range(len(dims))])
    return gain


def different_ones(own_key, rows, count, top, lift):
    sequence = jax.random.permutation(jax.random.fold_in(own_key, 1), count)
    pull = sequence
    for power in range(3):
        pull = pull * pull // count
    pull = pull * lift // count
    lots = jax.random.randint(jax.random.fold_in(own_key, 2), (rows, count), 0, 4096) + pull
    holders = jax.random.permutation(jax.random.fold_in(own_key, 3), rows)[jnp.arange(count) % rows]
    lots = jnp.where(jnp.arange(rows)[:, None] == holders[None, :], 1 << 14, lots)
    merit = lots * count + jnp.arange(count)
    return lax.top_k(merit.astype(jnp.int32), top)[1].astype(jnp.int32)


def deal_out(stream_key, own, number, rows, amount, top, limit, lean):
    order = jax.random.permutation(stream_key, amount)
    packed, usual = shares(amount, rows * top, limit, lean, True), shares(amount, rows * top, limit, lean, False)
    places = jnp.arange(amount)

    def named(tallies, offset_by):
        used = int((tallies > 0).sum())
        fixed = max(1, used // 4)
        moved = fixed + (places - fixed + offset_by * (used - fixed)) % max(1, amount - fixed)
        return jnp.zeros((amount,), jnp.int32).at[order[jnp.where(places < fixed, places, moved)]].set(jnp.asarray(tallies, jnp.int32))

    tallies = jnp.where(number % 4 == 0, named(packed, number // 4), named(usual, number - number // 4 - 1))
    mixed = jax.random.permutation(jax.random.fold_in(own, 3), amount)
    donor, taker = mixed[0:amount // 2 * 2:2], mixed[1:amount // 2 * 2:2]
    margin = jnp.minimum(tallies[donor] - 1, limit - tallies[taker]) // 2
    margin = jnp.where((donor == order[0]) | (taker == order[0]) | (tallies[taker] == 0), 0, jnp.maximum(margin, 0))
    moved = jax.random.randint(jax.random.fold_in(own, 4), (amount // 2,), 0, 1 << 20) % (margin + 1)
    tallies = tallies.at[donor].add(-moved).at[taker].add(moved)
    items = jnp.searchsorted(jnp.cumsum(tallies), jnp.arange(rows * top), side="right").astype(jnp.int32)
    table = items.reshape(top, rows).T
    table = table[jax.random.permutation(jax.random.fold_in(own, 1), rows)]
    offset_by = jax.random.randint(jax.random.fold_in(own, 2), (rows, 1), 0, top)
    return jnp.take_along_axis(table, (jnp.arange(top)[None, :] + offset_by) % top, axis=1)


def shares(amount, total, bound, slope, full):
    portions = [(1 << 20) // math.isqrt(rank ** slope) + 1 for rank in range(1, amount + 1)]
    largest = bound if full else min(bound, max(-(-total // amount), total * portions[0] // sum(portions)))
    least = 1 if total - largest >= amount - 1 else 0
    holding, spare = [largest] + [least] * (amount - 1), total - largest - least * (amount - 1)
    while spare > 0:
        free = [i for i in range(1, amount) if holding[i] < largest] or [i for i in range(1, amount) if holding[i] < bound]
        whole, left = sum([portions[i] for i in free]), spare
        for i in free:
            more = min(bound - holding[i], max(1, left * portions[i] // whole), spare)
            holding[i] = holding[i] + more
            spare = spare - more
    return np.array(holding)


def gaussian(stream_key, dims, width, limit, split=(), kind=jnp.bfloat16):
    drawn = jax.random.normal(stream_key, dims, jnp.float32) * width
    if len(split) > 0:
        drawn = level_of(stream_key, dims, split, -0.22, 0.18) * drawn
    return jnp.clip(drawn, min=-limit, max=limit).astype(kind)


def setup_inputs(seed: int = 0) -> dict:
    streams_of = jax.random.split(jax.random.key(seed), 11)
    orbitals = gaussian(streams_of[0], (BATCHES, PTS, BORB), 1.0, 6.0, ((0, 32),))
    dens_tiles = gaussian(streams_of[1], (TILES, TB, TB), (1.0 / BORB), 0.005859375, ((0, 32),))
    point_coords = jnp.clip(64.0 * jax.random.uniform(streams_of[2], (3, POINTS), jnp.float32) ** level_of(streams_of[2], (3, POINTS), ((1, 32),), -0.2, 0.2), 0.0, 64.0)
    point_weights = jnp.clip(jnp.exp(math.log(0.05) - 2.3025851 * jax.random.uniform(streams_of[3], (POINTS,), jnp.float32) ** level_of(streams_of[3], (POINTS,), ((0, 32),), -0.2, 0.2)), 0.005, 0.05)
    batch_blocks = different_ones(streams_of[4], BATCHES, UB, BB, 0)
    tile_owner_keys = jax.random.split(jax.random.fold_in(streams_of[5], 1), REQS // R)
    tile_owner_turns = jax.random.permutation(jax.random.fold_in(streams_of[5], 3), REQS // R)
    tile_owner = jax.vmap(lambda own, number: deal_out(jax.random.fold_in(streams_of[5], 2), own, number, R, OWNERS, 1, CAP, 1))(tile_owner_keys, tile_owner_turns).reshape((REQS, 1))
    tile_slot = with_ends(jax.random.randint(streams_of[6], (REQS,), 0, TILE_DEV), jax.random.fold_in(streams_of[6], 1), 0, TILE_DEV - 1).astype(jnp.int32)
    batch_atoms = different_ones(streams_of[7], BATCHES, ATOM_GRP, NEAR, 0)
    batch_weights = with_ends(jax.random.randint(streams_of[8], (BATCHES, NEAR), 1, 9), jax.random.fold_in(streams_of[8], 1), 1, 8).astype(jnp.int32)
    atom_grid_index = with_ends(jax.random.randint(streams_of[9], (3, ATOMS), 0, GRIDN), jax.random.fold_in(streams_of[9], 1), 0, GRIDN - 1).astype(jnp.int32)
    return dict(orbitals=orbitals, dens_tiles=dens_tiles, point_coords=point_coords, point_weights=point_weights, batch_blocks=batch_blocks, tile_owner=tile_owner, tile_slot=tile_slot, batch_atoms=batch_atoms, batch_weights=batch_weights, atom_grid_index=atom_grid_index)


TOP_PRECISION = lax.Precision.HIGHEST


def wave_table(count):
    mode_ids = jnp.arange(count // 2, dtype=jnp.int32)
    return jnp.stack([mode_ids % 8, (mode_ids // 8) % 8, mode_ids // 64]).astype(jnp.float32)


def kernel_gains(count):
    wave_vecs = wave_table(count)
    squared = jnp.sum(wave_vecs * wave_vecs, axis=0)
    near_gain = 0.1 / (1.0 + 0.1 * squared)
    far_gain = 0.03 / (1.0 + 0.1 * squared)
    return jnp.concatenate([near_gain, near_gain]), jnp.concatenate([far_gain, far_gain])


def local_basis(coords, centre_points, wave_vecs, grid_extent):
    displace = coords[:, :, None, :] - centre_points[:, :, :, None]
    phases = jnp.einsum("cbnp,cm->bnpm", displace, wave_vecs, precision=TOP_PRECISION) * (2.0 * math.pi / grid_extent)
    envelope = jnp.exp(-2.0 * jnp.sum(displace * displace, axis=0) / (grid_extent * grid_extent))
    return envelope[..., None] * jnp.concatenate([jnp.cos(phases), jnp.sin(phases)], axis=-1)


def wave_values(coords, wave_vecs, grid_extent):
    phases = jnp.einsum("cbp,cm->bpm", coords, wave_vecs, precision=TOP_PRECISION) * (2.0 * math.pi / grid_extent)
    return jnp.concatenate([jnp.cos(phases), jnp.sin(phases)], axis=-1)


def reference(orbitals, dens_tiles, point_coords, point_weights, batch_blocks, tile_owner, tile_slot, batch_atoms, batch_weights, atom_grid_index):
    devices = N_GRP * N_DEV
    wave_vecs = wave_table(KM)
    near_gain, far_gain = kernel_gains(KM)
    atom_location = atom_grid_index.astype(jnp.float32)
    group_of = jnp.arange(devices, dtype=jnp.int32) // N_DEV
    tile_index = (group_of[:, None] * (TILE_DEV * N_DEV) + tile_owner[:, 0].reshape(devices, R) * TILE_DEV
                  + tile_slot.reshape(devices, R)).astype(jnp.int32)
    orbital_dev = orbitals.reshape(devices, BAT_DEV, PTS, BORB)
    coord_dev = point_coords.reshape(3, devices, BAT_DEV, PTS)
    weight_dev = point_weights.reshape(devices, BAT_DEV, PTS)
    block_dev = batch_blocks.reshape(devices, BAT_DEV, BB)
    atom_dev = (batch_atoms.reshape(devices, BAT_DEV, NEAR) + group_of[:, None, None] * ATOM_GRP).astype(jnp.int32)
    raw_weight = batch_weights.reshape(devices, BAT_DEV, NEAR).astype(jnp.float32)
    partition = raw_weight / jnp.sum(raw_weight, axis=2, keepdims=True)
    device_ids = jnp.arange(devices, dtype=jnp.int32)
    batch_ids = jnp.arange(BAT_DEV, dtype=jnp.int32)

    def basis_of(device):
        return local_basis(coord_dev[:, device], atom_location[:, atom_dev[device]], wave_vecs, GRIDN)

    def density_pass(moments, device):
        local_tiles = dens_tiles[tile_index[device]]

        def one_batch(batch_no):
            orbital = orbital_dev[device, batch_no]
            chosen = block_dev[device, batch_no]
            block_index = chosen[:, None] * UB + chosen[None, :]
            dens_block = local_tiles[block_index].transpose(0, 2, 1, 3).reshape(BORB, BORB)
            product = jnp.dot(orbital, dens_block, preferred_element_type=jnp.float32)
            return jnp.sum(product * orbital.astype(jnp.float32), axis=1)

        density = lax.map(one_batch, batch_ids)
        ebasis = basis_of(device)
        coeffs = partition[device][:, :, None] * jnp.einsum("bp,bnpk->bnk", weight_dev[device] * density, ebasis, precision=TOP_PRECISION)
        moments = moments.at[atom_dev[device].reshape(-1)].add(coeffs.reshape(BAT_DEV * NEAR, KM))
        return moments, density

    moments, density_all = lax.scan(density_pass, jnp.zeros((ATOMS, KM), jnp.float32), device_ids)
    atom_trig = wave_values(atom_location[:, None, :], wave_vecs, GRIDN)[0]
    structure = jnp.dot(moments[:, 0], atom_trig, precision=TOP_PRECISION)
    coef_near = near_gain[None, :] * moments
    far_coef = far_gain * structure

    def hamilton_pass(ham_sum, device):
        ebasis = basis_of(device)
        chosen_coef = coef_near[atom_dev[device]]
        near_val = jnp.sum(partition[device][:, :, None] * jnp.einsum("bnpk,bnk->bnp", ebasis, chosen_coef, precision=TOP_PRECISION), axis=1)
        far_val = jnp.einsum("bpk,k->bp", wave_values(coord_dev[:, device], wave_vecs, GRIDN), far_coef, precision=TOP_PRECISION)
        potential = near_val + far_val
        scaled_pot = weight_dev[device] * potential

        def one_batch(ham_local, batch_no):
            orbital = orbital_dev[device, batch_no]
            chosen = block_dev[device, batch_no]
            scaled_orb = (scaled_pot[batch_no][:, None] * orbital.astype(jnp.float32)).astype(jnp.bfloat16)
            ham_batch = lax.dot_general(orbital, scaled_orb, (((0,), (0,)), ((), ())), preferred_element_type=jnp.float32)
            pieces = ham_batch.reshape(BB, TB, BB, TB).transpose(0, 2, 1, 3).reshape(BB * BB, TB, TB)
            block_index = (chosen[:, None] * UB + chosen[None, :]).reshape(-1)
            return ham_local.at[block_index].add(pieces), None

        ham_local, unused = lax.scan(one_batch, jnp.zeros((R, TB, TB), jnp.float32), batch_ids)
        rounded = lax.optimization_barrier(ham_local.astype(jnp.bfloat16)).astype(jnp.float32)
        return ham_sum.at[tile_index[device]].add(rounded), potential

    ham_sum, potential_all = lax.scan(hamilton_pass, jnp.zeros((TILES, TB, TB), jnp.float32), device_ids)
    return density_all.reshape(-1), potential_all.reshape(-1), ham_sum.astype(jnp.bfloat16)
```

```python
import functools
import math

import jax
import jax.numpy as jnp
from jax import lax
from jax.experimental import pallas as pl
from jax.experimental.pallas import tpu as pltpu
from jax.sharding import PartitionSpec as P

TB = 128
KM = 512
GRIDN = 64
HALF = KM // 2
MESH = pl.DeviceIdType.MESH
TOP = lax.Precision.HIGHEST
VM = pl.BlockSpec(memory_space=pltpu.VMEM)
SM = pl.BlockSpec(memory_space=pltpu.SMEM)
ANY = pl.BlockSpec(memory_space=pl.ANY)


def modes(shape, axis):
    k = lax.broadcasted_iota(jnp.int32, shape, axis)
    return tuple(v.astype(jnp.float32) for v in (k & 7, (k >> 3) & 7, k >> 6))


def turn_trig(turns):
    angle = (turns - jnp.round(turns)) * (2.0 * math.pi)
    return jnp.cos(angle), jnp.sin(angle)


def gather_kernel(
    n, orb, meta, coords, atoms_s, weights_s, grid_s,
    orb_all, meta_all, table, phase, spread,
    turns, own_sem, send, recv, msend, mrecv,
):
    me = lax.axis_index("dev")
    bits = n.bit_length() - 1
    batches, points = orb.shape[0], orb.shape[1]
    barrier = pltpu.get_barrier_semaphore()
    for step in range(1, n):
        pl.semaphore_signal(
            barrier, inc=1, device_id={"dev": lax.rem(me + step, n)}, device_id_type=MESH
        )
    pl.semaphore_wait(barrier, n - 1)

    def order_of(b):
        return list(range(bits)) if b % 2 == 0 else list(range(bits))[::-1]

    def block_copy(b, stage, mask):
        source = me ^ mask
        bit = 1 << order_of(b)[stage]
        got = mask ^ bit
        return pltpu.make_async_remote_copy(
            src_ref=orb.at[b] if mask == 0 else orb_all.at[source, b],
            dst_ref=orb_all.at[source, b],
            send_sem=send.at[b, got],
            recv_sem=recv.at[b, got],
            device_id={"dev": me ^ bit},
            device_id_type=MESH,
        )

    started = []
    metas = []
    for step in range(1, n):
        metas.append(
            pltpu.make_async_remote_copy(
                src_ref=meta,
                dst_ref=meta_all.at[me],
                send_sem=msend.at[step - 1],
                recv_sem=mrecv.at[step - 1],
                device_id={"dev": lax.rem(me + step, n)},
                device_id_type=MESH,
            )
        )
        metas[-1].start()
    for stage in range(bits):
        for b in range(batches):
            copy = block_copy(b, stage, 0)
            copy.start()
            started.append(copy)
    own = [
        pltpu.make_async_copy(orb, orb_all.at[me], own_sem.at[0]),
        pltpu.make_async_copy(meta, meta_all.at[me], own_sem.at[1]),
    ]
    for copy in own:
        copy.start()

    rows = 32

    def table_rows(c, carry):
        shape = (rows, batches * points)
        k = lax.broadcasted_iota(jnp.int32, shape, 0) + c * rows
        fx, fy, fz = (v.astype(jnp.float32) for v in (k & 7, (k >> 3) & 7, k >> 6))
        at = fx * coords[0:1, :] + fy * coords[1:2, :] + fz * coords[2:3, :]
        cos, sin = turn_trig(at * (1.0 / GRIDN))
        table[pl.ds(pl.multiple_of(c * rows, rows), rows), :] = cos
        table[pl.ds(pl.multiple_of(HALF + c * rows, rows), rows), :] = sin
        return carry

    def small_tables():
        atoms = grid_s.shape[1]
        turns[...] = jnp.zeros_like(turns)
        spread[...] = jnp.zeros_like(spread)
        fx, fy, fz = modes((1, HALF), 1)
        for a in range(atoms):
            place = [grid_s[c, a].astype(jnp.float32) for c in range(3)]
            turns[a : a + 1, :] = (fx * place[0] + fy * place[1] + fz * place[2]) * (1.0 / GRIDN)
            for b in range(batches):
                cols = slice(b * points, (b + 1) * points)
                share, total = jnp.int32(0), jnp.int32(0)
                for near in range(atoms_s.shape[1]):
                    weight = weights_s[b, near]
                    share = share + jnp.where(atoms_s[b, near] == a, weight, 0)
                    total = total + weight
                gone = [coords[c : c + 1, cols] - place[c] for c in range(3)]
                squared = gone[0] * gone[0] + gone[1] * gone[1] + gone[2] * gone[2]
                part = jnp.full((1, points), share.astype(jnp.float32)) / jnp.full(
                    (1, points), total.astype(jnp.float32)
                )
                spread[a : a + 1, cols] = part * jnp.exp(squared * (-2.0 / (GRIDN * GRIDN)))
        cos, sin = turn_trig(turns[...])
        phase[0] = cos
        phase[1] = sin

    small_tables()
    half_chunks = HALF // rows // 2
    lax.fori_loop(0, half_chunks, table_rows, 0)
    for stage in range(bits):
        for b in range(batches):
            for low in range(1 << stage):
                got = 1 << order_of(b)[stage]
                for t in range(stage):
                    if low >> t & 1:
                        got ^= 1 << order_of(b)[t]
                arrival = orb_all.at[me ^ got, b]
                pltpu.make_async_remote_copy(
                    src_ref=arrival,
                    dst_ref=arrival,
                    send_sem=send.at[b, got],
                    recv_sem=recv.at[b, got],
                    device_id={"dev": me ^ (1 << order_of(b)[stage])},
                    device_id_type=MESH,
                ).wait_recv()
                for later in range(stage + 1, bits):
                    copy = block_copy(b, later, got)
                    copy.start()
                    started.append(copy)
        if stage == 0:
            lax.fori_loop(half_chunks, HALF // rows, table_rows, 0)
    for copy in started:
        copy.wait_send()
    for copy in metas:
        copy.wait()
    for copy in own:
        copy.wait()


def density_kernel(meta, orb, dens, out, tiles, block, sem):
    e = pl.program_id(0)
    me = lax.axis_index("dev")
    stored = dens.shape[0]
    batches, points, width = orb.shape[1:]
    blocks = width // TB

    @pl.when(e == 0)
    def _():
        tiles[stored] = jnp.zeros((TB, TB), jnp.bfloat16)
        copy = pltpu.make_async_copy(dens, tiles.at[pl.ds(0, stored)], sem)
        copy.start()
        copy.wait()

    union = meta[0, 2, 0]
    for b in range(batches):

        def row(i, carry):
            ci = meta[e, 1, b * blocks + i]
            for j in range(blocks):
                code = meta[e, 0, ci * union + meta[e, 1, b * blocks + j]] - me * stored
                index = jnp.where((code >= 0) & (code < stored), code, stored)
                block[pl.ds(pl.multiple_of(i * TB, TB), TB), j * TB : (j + 1) * TB] = tiles[index]
            return carry

        lax.fori_loop(0, blocks, row, 0)
        total = jnp.zeros((points, TB), jnp.float32)
        for c in range(width // (2 * TB)):
            cols = slice(2 * c * TB, 2 * (c + 1) * TB)
            product = jnp.dot(orb[0, b], block[:, cols], preferred_element_type=jnp.float32)
            product = product * orb[0, b, :, cols].astype(jnp.float32)
            total = total + product[:, :TB] + product[:, TB:]
        line = jnp.sum(total.T, axis=0, keepdims=True)
        out[0, :, b * points : (b + 1) * points] = jnp.broadcast_to(line, (8, points))


def field_kernel(
    n, regions, dens, weights, table, phase, spread,
    density, potential, scaled_all,
    dens_in, terms, terms_in, struct, struct_in, scaled,
    dsend, drecv, tsend, trecv, ssend, srecv, psend, precv, own_sem,
):
    me = lax.axis_index("dev")
    grp = lax.axis_index("grp")
    barrier = pltpu.get_barrier_semaphore()
    for step in range(1, n):
        pl.semaphore_signal(
            barrier, inc=1, device_id={"dev": lax.rem(me + step, n)}, device_id_type=MESH
        )
    for step in range(1, regions):
        pl.semaphore_signal(
            barrier, inc=1, device_id={"grp": lax.rem(grp + step, regions)}, device_id_type=MESH
        )
    pl.semaphore_wait(barrier, n + regions - 2)

    def send_all(axis, count, src_of, dst_of, ssem, rsem):
        here = me if axis == "dev" else grp
        copies = []
        for step in range(1, count):
            peer = lax.rem(here + step, count)
            copies.append(
                pltpu.make_async_remote_copy(
                    src_ref=src_of(peer),
                    dst_ref=dst_of(step - 1),
                    send_sem=ssem.at[step - 1],
                    recv_sem=rsem.at[step - 1],
                    device_id={axis: peer},
                    device_id_type=MESH,
                )
            )
            copies[-1].start()
        return copies

    copies = send_all("dev", n, lambda peer: dens.at[peer], lambda s: dens_in.at[s], dsend, drecv)
    cos, sin = phase[0], phase[1]
    fx, fy, fz = modes((1, HALF), 1)
    squared = fx * fx + fy * fy + fz * fz
    near_gain = 0.1 / (1.0 + 0.1 * squared)
    far_gain = 0.03 / (1.0 + 0.1 * squared)
    rho = dens[me]
    for s, copy in enumerate(copies):
        copy.wait()
        rho = rho + dens_in[s]
    density[...] = rho
    source = spread[...] * (weights[...] * rho[0:1, :])
    mine = lax.dot_general(
        source, table[...], (((1,), (1,)), ((), ())), precision=TOP,
        preferred_element_type=jnp.float32,
    )
    terms[...] = mine
    copies = send_all("dev", n, lambda peer: terms, lambda s: terms_in.at[s], tsend, trecv)
    for s, copy in enumerate(copies):
        copy.wait()
        mine = mine + terms_in[s]
    even, odd = mine[:, :HALF], mine[:, HALF:]
    even, odd = even * cos + odd * sin, odd * cos - even * sin
    charge = even[:, 0:1]
    mine_struct = jnp.concatenate(
        [
            jnp.sum(charge * cos, axis=0, keepdims=True),
            jnp.sum(charge * sin, axis=0, keepdims=True),
        ],
        axis=1,
    )
    total = jnp.broadcast_to(mine_struct, (8, KM))
    struct[...] = total
    copies = send_all("grp", regions, lambda peer: struct, lambda s: struct_in.at[s], ssend, srecv)
    even, odd = even * near_gain, odd * near_gain
    coef = jnp.concatenate([even * cos - odd * sin, even * sin + odd * cos], axis=1)
    value = jnp.dot(coef, table[...], precision=TOP, preferred_element_type=jnp.float32)
    near = jnp.sum(value * spread[...], axis=0, keepdims=True)
    for s, copy in enumerate(copies):
        copy.wait()
        total = total + struct_in[s]
    far_coef = total * jnp.concatenate([far_gain, far_gain], axis=1)
    far = jnp.dot(far_coef, table[...], precision=TOP, preferred_element_type=jnp.float32)
    field = near + far
    potential[...] = field
    scaled[...] = weights[...] * field
    own = pltpu.make_async_copy(scaled, scaled_all.at[me], own_sem)
    own.start()
    copies = []
    for step in range(1, n):
        copies.append(
            pltpu.make_async_remote_copy(
                src_ref=scaled,
                dst_ref=scaled_all.at[me],
                send_sem=psend.at[step - 1],
                recv_sem=precv.at[step - 1],
                device_id={"dev": lax.rem(me + step, n)},
                device_id_type=MESH,
            )
        )
        copies[-1].start()
    for copy in copies:
        copy.wait()
    own.wait()


def hamilton_kernel(meta, orb, scaled, out, total, scaled_orb, block):
    e = pl.program_id(0)
    me = lax.axis_index("dev")
    stored = out.shape[0]
    batches, points, width = orb.shape[1:]
    blocks = width // TB

    @pl.when(e == 0)
    def _():
        total[...] = jnp.zeros_like(total)

    union = meta[0, 2, 0]
    for b in range(batches):
        line = scaled[0, 0:1, b * points : (b + 1) * points]
        column = jnp.broadcast_to(line, (TB, points)).T
        for j in range(blocks):
            cols = slice(j * TB, (j + 1) * TB)
            scaled_orb[:, cols] = (column * orb[0, b, :, cols].astype(jnp.float32)).astype(
                jnp.bfloat16
            )
        for c in range(width // (2 * TB)):
            cols = slice(2 * c * TB, 2 * (c + 1) * TB)
            block[:, cols] = lax.dot_general(
                orb[0, b], scaled_orb[:, cols], (((0,), (0,)), ((), ())),
                preferred_element_type=jnp.float32,
            )

        def row(i, carry):
            ci = meta[e, 1, b * blocks + i]
            for j in range(blocks):
                code = meta[e, 0, ci * union + meta[e, 1, b * blocks + j]] - me * stored

                @pl.when((code >= 0) & (code < stored))
                def _():
                    piece = block[pl.ds(pl.multiple_of(i * TB, TB), TB), j * TB : (j + 1) * TB]
                    total[code] = total[code] + piece

            return carry

        lax.fori_loop(0, blocks, row, 0)

    @pl.when(e == pl.num_programs(0) - 1)
    def _():
        out[...] = total[...].astype(jnp.bfloat16)


def on_device(
    n, regions, orbitals, dens_tiles, point_coords, point_weights, batch_blocks,
    tile_owner, tile_slot, batch_atoms, batch_weights, atom_grid_index,
):
    stored = dens_tiles.shape[0]
    listed = tile_slot.shape[0]
    batches, points, width = orbitals.shape
    here = batches * points
    rows = -(-atom_grid_index.shape[1] // 8) * 8
    code = tile_owner[:, 0] * stored + tile_slot
    meta = jnp.concatenate(
        [
            jnp.pad(code, (0, TB - listed))[None],
            jnp.pad(batch_blocks.reshape(-1), (0, TB - batch_blocks.size))[None],
            jnp.full((6, TB), math.isqrt(listed), jnp.int32),
        ]
    )
    f32, i32, bf16 = jnp.float32, jnp.int32, jnp.bfloat16
    S = jax.ShapeDtypeStruct
    dma = pltpu.SemaphoreType.DMA
    orb_all, meta_all, table, phase, spread = pl.pallas_call(
        functools.partial(gather_kernel, n),
        out_shape=(
            S((n, batches, points, width), bf16),
            S((n, 8, TB), i32),
            S((KM, here), f32),
            S((2, rows, HALF), f32),
            S((rows, here), f32),
        ),
        in_specs=[VM, VM, VM, SM, SM, SM],
        out_specs=(ANY, ANY, VM, VM, VM),
        scratch_shapes=[
            pltpu.VMEM((rows, HALF), f32),
            dma((2,)),
            dma((batches, n)),
            dma((batches, n)),
            dma((n,)),
            dma((n,)),
        ],
        compiler_params=pltpu.CompilerParams(collective_id=0, has_side_effects=True),
        name="gather",
    )(orbitals, meta, point_coords, batch_atoms, batch_weights, atom_grid_index)
    orb_spec = pl.BlockSpec((1, batches, points, width), lambda e: (e, 0, 0, 0))
    row_spec = pl.BlockSpec((1, 8, here), lambda e: (e, 0, 0))
    dens_part = pl.pallas_call(
        density_kernel,
        grid=(n,),
        out_shape=S((n, 8, here), f32),
        in_specs=[SM, orb_spec, ANY],
        out_specs=row_spec,
        scratch_shapes=[
            pltpu.VMEM((stored + 1, TB, TB), bf16),
            pltpu.VMEM((width, width), bf16),
            dma,
        ],
        name="density",
    )(meta_all, orb_all, dens_tiles)
    density, potential, scaled_all = pl.pallas_call(
        functools.partial(field_kernel, n, regions),
        out_shape=(S((8, here), f32), S((8, here), f32), S((n, 8, here), f32)),
        in_specs=[VM] * 5,
        out_specs=(VM, VM, VM),
        scratch_shapes=[
            pltpu.VMEM((n, 8, here), f32),
            pltpu.VMEM((rows, KM), f32),
            pltpu.VMEM((n, rows, KM), f32),
            pltpu.VMEM((8, KM), f32),
            pltpu.VMEM((regions, 8, KM), f32),
            pltpu.VMEM((8, here), f32),
            dma((n,)), dma((n,)), dma((n,)), dma((n,)),
            dma((regions,)), dma((regions,)), dma((n,)), dma((n,)), dma,
        ],
        compiler_params=pltpu.CompilerParams(collective_id=1, has_side_effects=True),
        name="field",
    )(dens_part, point_weights.reshape(1, here), table, phase, spread)
    ham_tiles = pl.pallas_call(
        hamilton_kernel,
        grid=(n,),
        out_shape=S((stored, TB, TB), bf16),
        in_specs=[SM, orb_spec, row_spec],
        out_specs=VM,
        scratch_shapes=[
            pltpu.VMEM((stored, TB, TB), f32),
            pltpu.VMEM((points, width), bf16),
            pltpu.VMEM((width, width), f32),
        ],
        name="hamilton",
    )(meta_all, orb_all, scaled_all)
    return density[0], potential[0], ham_tiles


def solution(mesh):
    body = functools.partial(on_device, mesh.shape["dev"], mesh.shape["grp"])
    in_specs = (
        P(("grp", "dev"), None, None),
        P(("grp", "dev"), None, None),
        P(None, ("grp", "dev")),
        P(("grp", "dev")),
        P(("grp", "dev"), None),
        P(("grp", "dev"), None),
        P(("grp", "dev")),
        P(("grp", "dev"), None),
        P(("grp", "dev"), None),
        P(None, "grp"),
    )
    out_specs = (P(("grp", "dev")), P(("grp", "dev")), P(("grp", "dev"), None, None))
    return jax.shard_map(body, mesh=mesh, in_specs=in_specs, out_specs=out_specs, check_vma=False)
```

```python
import functools
import math

import jax
import jax.numpy as jnp
from jax import lax
from jax.experimental import pallas as pl
from jax.experimental.pallas import tpu as pltpu
from jax.sharding import PartitionSpec as P

TB = 128
KM = 512
GRIDN = 64
HALF = KM // 2
MESH = pl.DeviceIdType.MESH
TOP = lax.Precision.HIGHEST
VM = pl.BlockSpec(memory_space=pltpu.VMEM)
SM = pl.BlockSpec(memory_space=pltpu.SMEM)
ANY = pl.BlockSpec(memory_space=pl.ANY)


def modes(shape, axis):
    k = lax.broadcasted_iota(jnp.int32, shape, axis)
    return tuple(v.astype(jnp.float32) for v in (k & 7, (k >> 3) & 7, k >> 6))


def turn_trig(turns):
    angle = (turns - jnp.round(turns)) * (2.0 * math.pi)
    return jnp.cos(angle), jnp.sin(angle)


def region_kernel(
    n, regions, orb, meta, coords, weights, dens, atoms_s, weights_s, grid_s,
    density, potential, scaled_all, meta_all, union_all, flip_all,
    table, phase, spread, turns, tiles, block, union, flip, part, part_in,
    terms, terms_in, struct, struct_in, scaled, meta_s,
    pack_sem, local_sem, send, recv, msend, mrecv, dsend, drecv, tsend, trecv, ssend, srecv, psend, precv,
    usem, fsem, *land,
):
    me = lax.axis_index("dev")
    grp = lax.axis_index("grp")
    bits = n.bit_length() - 1
    batches, points, width = orb.shape
    stored = dens.shape[0]
    blocks = union.shape[2] // TB
    held = width // TB
    packs = []
    for b in range(batches):
        for u in range(held):
            copy = pltpu.make_async_copy(
                orb.at[b, :, pl.ds(u * TB, TB)], land[0].at[b, u], pack_sem.at[b, u]
            )
            copy.start()
            packs.append(copy)
    for ref in land:
        for b in range(batches):
            ref[b, held] = jnp.zeros((points, TB), jnp.bfloat16)

    def clear(t, carry):
        tiles[t] = jnp.zeros((TB, TB), jnp.bfloat16)
        return carry

    lax.fori_loop(0, n * stored, clear, 0)
    for copy in packs:
        copy.wait()
    barrier = pltpu.get_barrier_semaphore()
    for mask in range(1, n):
        pl.semaphore_signal(barrier, inc=1, device_id={"dev": me ^ mask}, device_id_type=MESH)
    for step in range(1, regions):
        pl.semaphore_signal(
            barrier, inc=1, device_id={"grp": lax.rem(grp + step, regions)}, device_id_type=MESH
        )
    pl.semaphore_wait(barrier, n + regions - 2)

    def remote(src, dst, ssem, rsem, **where):
        return pltpu.make_async_remote_copy(
            src_ref=src, dst_ref=dst, send_sem=ssem, recv_sem=rsem,
            device_id=where, device_id_type=MESH,
        )

    def to_peers(src_of, dst_of, ssem, rsem):
        copies = []
        for mask in range(1, n):
            copy = remote(src_of(mask), dst_of(mask), ssem.at[mask], rsem.at[mask], dev=me ^ mask)
            copy.start()
            copies.append(copy)
        return copies

    def order_of(b):
        return list(range(bits)) if b % 2 == 0 else list(range(bits))[::-1]

    def landing(mask, b):
        return land[mask].at[b, pl.ds(0, held)]

    def block_copy(b, stage, mask):
        bit = 1 << order_of(b)[stage]
        got = mask ^ bit
        return remote(landing(mask, b), landing(got, b), send.at[b, got], recv.at[b, got], dev=me ^ bit)

    started = []
    metas = to_peers(lambda mask: meta, lambda mask: meta_all.at[me], msend, mrecv)
    for stage in range(bits):
        for b in range(batches):
            copy = block_copy(b, stage, 0)
            copy.start()
            started.append(copy)
    own = [
        pltpu.make_async_copy(meta, meta_all.at[me], local_sem.at[0]),
        pltpu.make_async_copy(dens, tiles.at[pl.ds(me * stored, stored)], local_sem.at[1]),
    ]
    for copy in own:
        copy.start()

    rows = 32

    def table_rows(c, carry):
        shape = (rows, batches * points)
        k = lax.broadcasted_iota(jnp.int32, shape, 0) + c * rows
        fx, fy, fz = (v.astype(jnp.float32) for v in (k & 7, (k >> 3) & 7, k >> 6))
        at = fx * coords[0:1, :] + fy * coords[1:2, :] + fz * coords[2:3, :]
        cos, sin = turn_trig(at * (1.0 / GRIDN))
        table[pl.ds(pl.multiple_of(c * rows, rows), rows), :] = cos
        table[pl.ds(pl.multiple_of(HALF + c * rows, rows), rows), :] = sin
        return carry

    def small_tables():
        atoms = grid_s.shape[1]
        turns[...] = jnp.zeros_like(turns)
        spread[...] = jnp.zeros_like(spread)
        fx, fy, fz = modes((1, HALF), 1)
        for a in range(atoms):
            place = [grid_s[c, a].astype(jnp.float32) for c in range(3)]
            turns[a : a + 1, :] = (fx * place[0] + fy * place[1] + fz * place[2]) * (1.0 / GRIDN)
            for b in range(batches):
                cols = slice(b * points, (b + 1) * points)
                share, total = jnp.int32(0), jnp.int32(0)
                for near in range(atoms_s.shape[1]):
                    weight = weights_s[b, near]
                    share = share + jnp.where(atoms_s[b, near] == a, weight, 0)
                    total = total + weight
                gone = [coords[c : c + 1, cols] - place[c] for c in range(3)]
                squared = gone[0] * gone[0] + gone[1] * gone[1] + gone[2] * gone[2]
                fraction = jnp.full((1, points), share.astype(jnp.float32)) / jnp.full(
                    (1, points), total.astype(jnp.float32)
                )
                spread[a : a + 1, cols] = fraction * jnp.exp(squared * (-2.0 / (GRIDN * GRIDN)))
        cos, sin = turn_trig(turns[...])
        phase[0] = cos
        phase[1] = sin

    results = {}
    density_sends = []

    def process(mask):
        e = me ^ mask
        slot = len(results) % 2
        if len(results) >= 2:
            for copy in list(results.values())[-2]:
                copy.wait()
        for b in range(batches):
            at = slice(b * points, (b + 1) * points)
            for u in range(blocks):
                index = meta_s[e, 1, b * blocks + u]
                union[slot, at, u * TB : (u + 1) * TB] = land[mask][b, index]

        def flip_block(u, carry):
            first = pl.multiple_of(u * TB, TB)
            flip[slot, pl.ds(first, TB), :] = union[slot, :, pl.ds(first, TB)].T
            return carry

        lax.fori_loop(0, blocks, flip_block, 0)
        outs = [
            pltpu.make_async_copy(union.at[slot], union_all.at[e], usem.at[mask]),
            pltpu.make_async_copy(flip.at[slot], flip_all.at[e], fsem.at[mask]),
        ]
        for copy in outs:
            copy.start()
        results[mask] = outs

        def row(i, carry):
            for j in range(blocks):
                index = meta_s[e, 0, i * blocks + j]
                block[pl.ds(pl.multiple_of(i * TB, TB), TB), j * TB : (j + 1) * TB] = tiles[index]
            return carry

        lax.fori_loop(0, blocks, row, 0)
        total = jnp.zeros((batches * points, TB), jnp.float32)
        for c in range(0, blocks, 2):
            some = min(2, blocks - c)
            cols = slice(c * TB, (c + some) * TB)
            orbital = union[slot, :, cols]
            product = jnp.dot(union[slot], block[:, cols], preferred_element_type=jnp.float32)
            product = product * orbital.astype(jnp.float32)
            for t in range(some):
                total = total + product[:, t * TB : (t + 1) * TB]
        line = jnp.sum(total.T, axis=0, keepdims=True)
        part[mask] = jnp.broadcast_to(line, (8, batches * points))
        if mask:
            copy = remote(
                part.at[mask], part_in.at[mask], dsend.at[mask], drecv.at[mask], dev=me ^ mask
            )
            copy.start()
            density_sends.append(copy)

    small_tables()
    chunks = HALF // rows
    lax.fori_loop(0, chunks // 2, table_rows, 0)
    for copy in metas + own:
        copy.wait()
    to_smem = pltpu.make_async_copy(meta_all, meta_s, local_sem.at[0])
    to_smem.start()
    to_smem.wait()
    process(0)
    arrived = {}
    for stage in range(bits):
        for low in range(1 << stage):
            for b in range(batches):
                bit = 1 << order_of(b)[stage]
                got = bit
                for t in range(stage):
                    if low >> t & 1:
                        got ^= 1 << order_of(b)[t]
                there = landing(got, b)
                remote(there, there, send.at[b, got], recv.at[b, got], dev=me ^ bit).wait_recv()
                for later in range(stage + 1, bits):
                    copy = block_copy(b, later, got)
                    copy.start()
                    started.append(copy)
                arrived[got] = arrived.get(got, 0) + 1
                if arrived[got] == batches:
                    process(got)
        if stage == 0:
            lax.fori_loop(chunks // 2, chunks, table_rows, 0)

    cos, sin = phase[0], phase[1]
    fx, fy, fz = modes((1, HALF), 1)
    squared = fx * fx + fy * fy + fz * fz
    near_gain = 0.1 / (1.0 + 0.1 * squared)
    far_gain = 0.03 / (1.0 + 0.1 * squared)
    rho = part[0]
    for copy in density_sends:
        copy.wait()
    for mask in range(1, n):
        rho = rho + part_in[mask]
    density[...] = rho
    source = spread[...] * (weights[...] * rho[0:1, :])
    mine = lax.dot_general(
        source, table[...], (((1,), (1,)), ((), ())), precision=TOP,
        preferred_element_type=jnp.float32,
    )
    terms[...] = mine
    copies = to_peers(lambda mask: terms, lambda mask: terms_in.at[mask], tsend, trecv)
    for mask, copy in enumerate(copies, 1):
        copy.wait()
        mine = mine + terms_in[mask]
    even, odd = mine[:, :HALF], mine[:, HALF:]
    even, odd = even * cos + odd * sin, odd * cos - even * sin
    charge = even[:, 0:1]
    total = jnp.concatenate(
        [
            jnp.sum(charge * cos, axis=0, keepdims=True),
            jnp.sum(charge * sin, axis=0, keepdims=True),
        ],
        axis=1,
    )
    total = jnp.broadcast_to(total, (8, KM))
    struct[...] = total
    copies = []
    for step in range(1, regions):
        copies.append(
            remote(
                struct, struct_in.at[step], ssend.at[step], srecv.at[step],
                grp=lax.rem(grp + step, regions),
            )
        )
        copies[-1].start()
    even, odd = even * near_gain, odd * near_gain
    coef = jnp.concatenate([even * cos - odd * sin, even * sin + odd * cos], axis=1)
    value = jnp.dot(coef, table[...], precision=TOP, preferred_element_type=jnp.float32)
    near = jnp.sum(value * spread[...], axis=0, keepdims=True)
    for step, copy in enumerate(copies, 1):
        copy.wait()
        total = total + struct_in[step]
    far_coef = total * jnp.concatenate([far_gain, far_gain], axis=1)
    far = jnp.dot(far_coef, table[...], precision=TOP, preferred_element_type=jnp.float32)
    field = near + far
    potential[...] = field
    scaled[...] = weights[...] * field
    keep = pltpu.make_async_copy(scaled, scaled_all.at[me], local_sem.at[0])
    keep.start()
    copies = to_peers(lambda mask: scaled, lambda mask: scaled_all.at[me], psend, precv)
    for outs in list(results.values())[-2:]:
        for copy in outs:
            copy.wait()
    for copy in started:
        copy.wait_send()
    for copy in copies:
        copy.wait()
    keep.wait()


def hamilton_kernel(
    meta, orb, orb_flip, scaled, density8, potential8, out, density, potential,
    total, scaled_orb, block, chosen,
):
    e = pl.program_id(0)
    me = lax.axis_index("dev")
    stored = out.shape[0]
    points, width = orb.shape[1:]
    blocks = width // TB

    @pl.when(e == 0)
    def _():
        total[...] = jnp.zeros_like(total)
        for q in range(points // TB):
            density[q : q + 1, :] = density8[0:1, q * TB : (q + 1) * TB]
            potential[q : q + 1, :] = potential8[0:1, q * TB : (q + 1) * TB]

    count = jnp.int32(0)
    for r in range(blocks * blocks):
        code = meta[e, 0, r] - me * stored
        chosen[count] = r
        count = count + ((code >= 0) & (code < stored)).astype(jnp.int32)
    column = jnp.broadcast_to(scaled[0, 0:1, :], (TB, points)).T
    for j in range(blocks):
        cols = slice(j * TB, (j + 1) * TB)
        scaled_orb[:, cols] = (column * orb[0, :, cols].astype(jnp.float32)).astype(jnp.bfloat16)
    for c in range(0, blocks, 2):
        some = min(2, blocks - c)
        product = jnp.dot(
            orb_flip[0], scaled_orb[:, c * TB : (c + some) * TB],
            preferred_element_type=jnp.float32,
        )
        for t in range(some):
            block[c + t] = product[:, t * TB : (t + 1) * TB]

    def add(q, carry):
        r = chosen[q]
        i = r // blocks
        slot = meta[e, 0, r] - me * stored
        piece = block[r - i * blocks, pl.ds(pl.multiple_of(i * TB, TB), TB), :]
        total[slot] = total[slot] + piece
        return carry

    lax.fori_loop(0, count, add, 0)

    @pl.when(e == pl.num_programs(0) - 1)
    def _():
        out[...] = total[...].astype(jnp.bfloat16)


def on_device(
    n, regions, orbitals, dens_tiles, point_coords, point_weights, batch_blocks,
    tile_owner, tile_slot, batch_atoms, batch_weights, atom_grid_index,
):
    stored = dens_tiles.shape[0]
    listed = tile_slot.shape[0]
    batches, points, width = orbitals.shape
    here = batches * points
    union = math.isqrt(listed)
    wide = union * TB
    rows = -(-atom_grid_index.shape[1] // 8) * 8
    code = tile_owner[:, 0] * stored + tile_slot
    blocks = width // TB
    hit = batch_blocks[:, None, :] == jnp.arange(union, dtype=jnp.int32)[None, :, None]
    place = blocks - jnp.sum(
        jnp.where(hit, blocks - jnp.arange(blocks, dtype=jnp.int32), 0), axis=2
    )
    meta = jnp.concatenate(
        [
            jnp.pad(code, (0, TB - listed))[None],
            jnp.pad(place.reshape(-1), (0, TB - batches * union))[None],
            jnp.zeros((6, TB), jnp.int32),
        ]
    )
    f32, i32, bf16 = jnp.float32, jnp.int32, jnp.bfloat16
    S = jax.ShapeDtypeStruct
    dma = pltpu.SemaphoreType.DMA
    V = pltpu.VMEM
    density, potential, scaled_all, meta_all, union_all, flip_all = pl.pallas_call(
        functools.partial(region_kernel, n, regions),
        out_shape=(
            S((8, here), f32),
            S((8, here), f32),
            S((n, 8, here), f32),
            S((n, 8, TB), i32),
            S((n, here, wide), bf16),
            S((n, wide, here), bf16),
        ),
        in_specs=[ANY, VM, VM, VM, ANY, SM, SM, SM],
        out_specs=(VM, VM, VM, ANY, ANY, ANY),
        scratch_shapes=[
            V((KM, here), f32),
            V((2, rows, HALF), f32),
            V((rows, here), f32),
            V((rows, HALF), f32),
            V((n * stored, TB, TB), bf16),
            V((wide, wide), bf16),
            V((2, here, wide), bf16),
            V((2, wide, here), bf16),
            V((n, 8, here), f32),
            V((n, 8, here), f32),
            V((rows, KM), f32),
            V((n, rows, KM), f32),
            V((8, KM), f32),
            V((regions, 8, KM), f32),
            V((8, here), f32),
            pltpu.SMEM((n, 8, TB), i32),
            dma((batches, blocks)),
            dma((2,)),
            dma((batches, n)), dma((batches, n)),
            dma((n,)), dma((n,)), dma((n,)), dma((n,)), dma((n,)), dma((n,)),
            dma((regions,)), dma((regions,)), dma((n,)), dma((n,)), dma((n,)), dma((n,)),
            *[V((batches, blocks + 1, points, TB), bf16) for _ in range(n)],
        ],
        compiler_params=pltpu.CompilerParams(collective_id=0, has_side_effects=True),
        name="region",
    )(
        orbitals, meta, point_coords, point_weights.reshape(1, here), dens_tiles,
        batch_atoms, batch_weights, atom_grid_index,
    )
    ham_tiles, density, potential = pl.pallas_call(
        hamilton_kernel,
        grid=(n,),
        out_shape=(
            S((stored, TB, TB), bf16), S((here // TB, TB), f32), S((here // TB, TB), f32),
        ),
        in_specs=[
            SM,
            pl.BlockSpec((1, here, wide), lambda e: (e, 0, 0)),
            pl.BlockSpec((1, wide, here), lambda e: (e, 0, 0)),
            pl.BlockSpec((1, 8, here), lambda e: (e, 0, 0)),
            VM,
            VM,
        ],
        out_specs=(VM, VM, VM),
        scratch_shapes=[
            V((stored, TB, TB), f32),
            V((here, wide), bf16),
            V((union, wide, TB), f32),
            pltpu.SMEM((listed + 1,), i32),
        ],
        name="hamilton",
    )(meta_all, union_all, flip_all, scaled_all, density, potential)
    return density.reshape(-1), potential.reshape(-1), ham_tiles


def solution(mesh):
    body = functools.partial(on_device, mesh.shape["dev"], mesh.shape["grp"])
    in_specs = (
        P(("grp", "dev"), None, None),
        P(("grp", "dev"), None, None),
        P(None, ("grp", "dev")),
        P(("grp", "dev")),
        P(("grp", "dev"), None),
        P(("grp", "dev"), None),
        P(("grp", "dev")),
        P(("grp", "dev"), None),
        P(("grp", "dev"), None),
        P(None, "grp"),
    )
    out_specs = (P(("grp", "dev")), P(("grp", "dev")), P(("grp", "dev"), None, None))
    return jax.shard_map(body, mesh=mesh, in_specs=in_specs, out_specs=out_specs, check_vma=False)
```

```python
import functools
import math

import jax
import jax.numpy as jnp
from jax import lax
from jax.experimental import pallas as pl
from jax.experimental.pallas import tpu as pltpu
from jax.sharding import PartitionSpec as P

TB = 128
KM = 512
GRIDN = 64
HALF = KM // 2
MESH = pl.DeviceIdType.MESH
VM = pl.BlockSpec(memory_space=pltpu.VMEM)
SM = pl.BlockSpec(memory_space=pltpu.SMEM)
ANY = pl.BlockSpec(memory_space=pl.ANY)


def modes(shape, axis):
    k = lax.broadcasted_iota(jnp.int32, shape, axis)
    return tuple(v.astype(jnp.float32) for v in (k & 7, (k >> 3) & 7, k >> 6))


def turn_trig(turns):
    angle = (turns - jnp.round(turns)) * (2.0 * math.pi)
    return jnp.cos(angle), jnp.sin(angle)


def split(value):
    high = value.astype(jnp.bfloat16)
    return high, (value - high.astype(jnp.float32)).astype(jnp.bfloat16)


def split_dot(value, table):
    rows = value.shape[0]
    high = value.astype(jnp.bfloat16)
    rest = value - high.astype(jnp.float32)
    both = jnp.concatenate([value, rest], axis=0).astype(jnp.bfloat16)
    out = jnp.dot(both, table[0], preferred_element_type=jnp.float32)
    return out[:rows] + out[rows:] + jnp.dot(high, table[1], preferred_element_type=jnp.float32)


def region_kernel(
    n, regions, orb, meta, coords, weights, dens, atoms_s, weights_s, grid_s,
    density, potential, scaled_all, meta_all, union_all, flip_all,
    table, table_t, phase, spread, turns, tiles, block, union, flip, part, part_in,
    terms, terms_in, struct, struct_in, scaled, meta_s,
    pack_sem, local_sem, send, recv, msend, mrecv, dsend, drecv, tsend, trecv, ssend, srecv, psend, precv,
    usem, fsem, *land,
):
    me = lax.axis_index("dev")
    grp = lax.axis_index("grp")
    bits = n.bit_length() - 1
    batches, points, width = orb.shape
    stored = dens.shape[0]
    blocks = union.shape[2] // TB
    held = width // TB
    packs = []
    for b in range(batches):
        for u in range(held):
            copy = pltpu.make_async_copy(
                orb.at[b, :, pl.ds(u * TB, TB)], land[0].at[b, u], pack_sem.at[b, u]
            )
            copy.start()
            packs.append(copy)
    barrier = pltpu.get_barrier_semaphore()
    for mask in range(1, n):
        pl.semaphore_signal(barrier, inc=1, device_id={"dev": me ^ mask}, device_id_type=MESH)
    for step in range(1, regions):
        pl.semaphore_signal(
            barrier, inc=1, device_id={"grp": lax.rem(grp + step, regions)}, device_id_type=MESH
        )
    for ref in land:
        for b in range(batches):
            ref[b, held] = jnp.zeros((points, TB), jnp.bfloat16)

    def clear(t, carry):
        tiles[t] = jnp.zeros((TB, TB), jnp.bfloat16)
        return carry

    lax.fori_loop(0, n * stored, clear, 0)
    for copy in packs:
        copy.wait()
    pl.semaphore_wait(barrier, n + regions - 2)

    def remote(src, dst, ssem, rsem, **where):
        return pltpu.make_async_remote_copy(
            src_ref=src, dst_ref=dst, send_sem=ssem, recv_sem=rsem,
            device_id=where, device_id_type=MESH,
        )

    def to_peers(src_of, dst_of, ssem, rsem):
        copies = []
        for mask in range(1, n):
            copy = remote(src_of(mask), dst_of(mask), ssem.at[mask], rsem.at[mask], dev=me ^ mask)
            copy.start()
            copies.append(copy)
        return copies

    def order_of(b):
        return list(range(bits)) if b % 2 == 0 else list(range(bits))[::-1]

    def landing(mask, b):
        return land[mask].at[b, pl.ds(0, held)]

    def block_copy(b, stage, mask):
        bit = 1 << order_of(b)[stage]
        got = mask ^ bit
        return remote(landing(mask, b), landing(got, b), send.at[b, got], recv.at[b, got], dev=me ^ bit)

    started = []
    metas = to_peers(lambda mask: meta, lambda mask: meta_all.at[me], msend, mrecv)
    for stage in range(bits):
        for b in range(batches):
            copy = block_copy(b, stage, 0)
            copy.start()
            started.append(copy)
    own = [
        pltpu.make_async_copy(meta, meta_all.at[me], local_sem.at[0]),
        pltpu.make_async_copy(dens, tiles.at[pl.ds(me * stored, stored)], local_sem.at[1]),
    ]
    for copy in own:
        copy.start()

    rows = 32

    def table_rows(c, carry):
        shape = (rows, batches * points)
        k = lax.broadcasted_iota(jnp.int32, shape, 0) + c * rows
        fx, fy, fz = (v.astype(jnp.float32) for v in (k & 7, (k >> 3) & 7, k >> 6))
        at = fx * coords[0:1, :] + fy * coords[1:2, :] + fz * coords[2:3, :]
        cos, sin = turn_trig(at * (1.0 / GRIDN))
        for first, wave in ((0, cos), (HALF, sin)):
            high, low = split(wave)
            at = pl.ds(pl.multiple_of(first + c * rows, rows), rows)
            table[0, at, :] = high
            table[1, at, :] = low
        return carry

    def turn_rows(c, carry):
        at = pl.ds(pl.multiple_of(c * TB, TB), TB)
        table_t[0, :, at] = table[0, at, :].T
        table_t[1, :, at] = table[1, at, :].T
        return carry

    def small_tables():
        atoms = grid_s.shape[1]
        turns[...] = jnp.zeros_like(turns)
        spread[...] = jnp.zeros_like(spread)
        fx, fy, fz = modes((1, HALF), 1)
        for a in range(atoms):
            place = [grid_s[c, a].astype(jnp.float32) for c in range(3)]
            turns[a : a + 1, :] = (fx * place[0] + fy * place[1] + fz * place[2]) * (1.0 / GRIDN)
            for b in range(batches):
                cols = slice(b * points, (b + 1) * points)
                share, total = jnp.int32(0), jnp.int32(0)
                for near in range(atoms_s.shape[1]):
                    weight = weights_s[b, near]
                    share = share + jnp.where(atoms_s[b, near] == a, weight, 0)
                    total = total + weight
                gone = [coords[c : c + 1, cols] - place[c] for c in range(3)]
                squared = gone[0] * gone[0] + gone[1] * gone[1] + gone[2] * gone[2]
                fraction = jnp.full((1, points), share.astype(jnp.float32)) / jnp.full(
                    (1, points), total.astype(jnp.float32)
                )
                spread[a : a + 1, cols] = fraction * jnp.exp(squared * (-2.0 / (GRIDN * GRIDN)))
        cos, sin = turn_trig(turns[...])
        phase[0] = cos
        phase[1] = sin

    results = {}
    density_sends = []

    def process(mask):
        e = me ^ mask
        slot = len(results) % 2
        if len(results) >= 2:
            for copy in list(results.values())[-2]:
                copy.wait()
        for b in range(batches):
            at = slice(b * points, (b + 1) * points)
            for u in range(blocks):
                index = meta_s[e, 1, b * blocks + u]
                union[slot, at, u * TB : (u + 1) * TB] = land[mask][b, index]

        total = jnp.zeros((batches * points, TB), jnp.float32)
        for c in range(0, blocks, 2):
            some = min(2, blocks - c)
            cols = slice(c * TB, (c + some) * TB)
            orbital = union[slot, :, cols]
            product = jnp.dot(union[slot], block[:, cols], preferred_element_type=jnp.float32)
            product = product * orbital.astype(jnp.float32)
            for t in range(some):
                total = total + product[:, t * TB : (t + 1) * TB]
        line = jnp.sum(total.T, axis=0, keepdims=True)
        part[mask] = jnp.broadcast_to(line, (8, batches * points))
        if mask:
            copy = remote(
                part.at[mask], part_in.at[mask], dsend.at[mask], drecv.at[mask], dev=me ^ mask
            )
            copy.start()
            density_sends.append(copy)

        def flip_block(u, carry):
            first = pl.multiple_of(u * TB, TB)
            flip[slot, pl.ds(first, TB), :] = union[slot, :, pl.ds(first, TB)].T
            return carry

        lax.fori_loop(0, blocks, flip_block, 0)
        outs = [
            pltpu.make_async_copy(union.at[slot], union_all.at[e], usem.at[mask]),
            pltpu.make_async_copy(flip.at[slot], flip_all.at[e], fsem.at[mask]),
        ]
        for copy in outs:
            copy.start()
        results[mask] = outs

    def assemble(mask):
        e = me ^ mask

        def row(i, carry):
            for j in range(blocks):
                index = meta_s[e, 0, i * blocks + j]
                block[pl.ds(pl.multiple_of(i * TB, TB), TB), j * TB : (j + 1) * TB] = tiles[index]
            return carry

        lax.fori_loop(0, blocks, row, 0)

    arrivals = []
    counts = {}
    order = [0]
    for stage in range(bits):
        for low in range(1 << stage):
            for b in range(batches):
                got = 1 << order_of(b)[stage]
                for t in range(stage):
                    if low >> t & 1:
                        got ^= 1 << order_of(b)[t]
                counts[got] = counts.get(got, 0) + 1
                arrivals.append((stage, b, got, counts[got] == batches))
                if counts[got] == batches:
                    order.append(got)
    order.append(None)
    small_tables()
    chunks = HALF // rows
    lax.fori_loop(0, chunks // 2, table_rows, 0)
    for copy in metas + own:
        copy.wait()
    to_smem = pltpu.make_async_copy(meta_all, meta_s, local_sem.at[0])
    to_smem.start()
    to_smem.wait()
    assemble(0)
    process(0)
    assemble(order[1])
    last = 0
    for stage, b, got, whole in arrivals:
        if stage != last:
            if last == 0:
                lax.fori_loop(chunks // 2, chunks, table_rows, 0)
                lax.fori_loop(0, KM // TB, turn_rows, 0)
            last = stage
        there = landing(got, b)
        bit = 1 << order_of(b)[stage]
        remote(there, there, send.at[b, got], recv.at[b, got], dev=me ^ bit).wait_recv()
        for later in range(stage + 1, bits):
            copy = block_copy(b, later, got)
            copy.start()
            started.append(copy)
        if whole:
            process(got)
            following = order[order.index(got) + 1]
            if following is not None:
                assemble(following)

    cos, sin = phase[0], phase[1]
    fx, fy, fz = modes((1, HALF), 1)
    squared = fx * fx + fy * fy + fz * fz
    near_gain = 0.1 / (1.0 + 0.1 * squared)
    far_gain = 0.03 / (1.0 + 0.1 * squared)
    rho = part[0]
    for copy in density_sends:
        copy.wait()
    for mask in range(1, n):
        rho = rho + part_in[mask]
    density[...] = rho
    source = spread[...] * (weights[...] * rho[0:1, :])
    mine = split_dot(source, table_t)
    terms[...] = mine
    copies = to_peers(lambda mask: terms, lambda mask: terms_in.at[mask], tsend, trecv)
    for mask, copy in enumerate(copies, 1):
        copy.wait()
        mine = mine + terms_in[mask]
    even, odd = mine[:, :HALF], mine[:, HALF:]
    even, odd = even * cos + odd * sin, odd * cos - even * sin
    charge = even[:, 0:1]
    total = jnp.concatenate(
        [
            jnp.sum(charge * cos, axis=0, keepdims=True),
            jnp.sum(charge * sin, axis=0, keepdims=True),
        ],
        axis=1,
    )
    total = jnp.broadcast_to(total, (8, KM))
    struct[...] = total
    copies = []
    for step in range(1, regions):
        copies.append(
            remote(
                struct, struct_in.at[step], ssend.at[step], srecv.at[step],
                grp=lax.rem(grp + step, regions),
            )
        )
        copies[-1].start()
    even, odd = even * near_gain, odd * near_gain
    coef = jnp.concatenate([even * cos - odd * sin, even * sin + odd * cos], axis=1)
    value = split_dot(coef, table)
    near = jnp.sum(value * spread[...], axis=0, keepdims=True)
    for step, copy in enumerate(copies, 1):
        copy.wait()
        total = total + struct_in[step]
    far_coef = total * jnp.concatenate([far_gain, far_gain], axis=1)
    far = split_dot(far_coef, table)
    field = near + far
    potential[...] = field
    scaled[...] = weights[...] * field
    keep = pltpu.make_async_copy(scaled, scaled_all.at[me], local_sem.at[0])
    keep.start()
    copies = to_peers(lambda mask: scaled, lambda mask: scaled_all.at[me], psend, precv)
    for outs in list(results.values())[-2:]:
        for copy in outs:
            copy.wait()
    for copy in started:
        copy.wait_send()
    for copy in copies:
        copy.wait()
    keep.wait()


def hamilton_kernel(
    meta, orb, orb_flip, scaled, density8, potential8, out, density, potential,
    total, scaled_orb, block, chosen,
):
    e = pl.program_id(0)
    me = lax.axis_index("dev")
    stored = out.shape[0]
    points, width = orb.shape[1:]
    blocks = width // TB

    @pl.when(e == 0)
    def _():
        total[...] = jnp.zeros_like(total)
        for q in range(points // TB):
            density[q : q + 1, :] = density8[0:1, q * TB : (q + 1) * TB]
            potential[q : q + 1, :] = potential8[0:1, q * TB : (q + 1) * TB]

    count = jnp.int32(0)
    for r in range(blocks * blocks):
        code = meta[e, 0, r] - me * stored
        chosen[count] = r
        count = count + ((code >= 0) & (code < stored)).astype(jnp.int32)
    column = jnp.broadcast_to(scaled[0, 0:1, :], (TB, points)).T
    for j in range(blocks):
        cols = slice(j * TB, (j + 1) * TB)
        scaled_orb[:, cols] = (column * orb[0, :, cols].astype(jnp.float32)).astype(jnp.bfloat16)
    for c in range(0, blocks, 2):
        some = min(2, blocks - c)
        product = jnp.dot(
            orb_flip[0], scaled_orb[:, c * TB : (c + some) * TB],
            preferred_element_type=jnp.float32,
        )
        for t in range(some):
            block[c + t] = product[:, t * TB : (t + 1) * TB]

    def add(q, carry):
        r = chosen[q]
        i = r // blocks
        slot = meta[e, 0, r] - me * stored
        piece = block[r - i * blocks, pl.ds(pl.multiple_of(i * TB, TB), TB), :]
        total[slot] = total[slot] + piece
        return carry

    lax.fori_loop(0, count, add, 0)

    @pl.when(e == pl.num_programs(0) - 1)
    def _():
        out[...] = total[...].astype(jnp.bfloat16)


def on_device(
    n, regions, orbitals, dens_tiles, point_coords, point_weights, batch_blocks,
    tile_owner, tile_slot, batch_atoms, batch_weights, atom_grid_index,
):
    stored = dens_tiles.shape[0]
    listed = tile_slot.shape[0]
    batches, points, width = orbitals.shape
    here = batches * points
    union = math.isqrt(listed)
    wide = union * TB
    rows = -(-atom_grid_index.shape[1] // 8) * 8
    code = tile_owner[:, 0] * stored + tile_slot
    blocks = width // TB
    hit = batch_blocks[:, None, :] == jnp.arange(union, dtype=jnp.int32)[None, :, None]
    place = blocks - jnp.sum(
        jnp.where(hit, blocks - jnp.arange(blocks, dtype=jnp.int32), 0), axis=2
    )
    meta = jnp.concatenate(
        [
            jnp.pad(code, (0, TB - listed))[None],
            jnp.pad(place.reshape(-1), (0, TB - batches * union))[None],
            jnp.zeros((6, TB), jnp.int32),
        ]
    )
    f32, i32, bf16 = jnp.float32, jnp.int32, jnp.bfloat16
    S = jax.ShapeDtypeStruct
    dma = pltpu.SemaphoreType.DMA
    V = pltpu.VMEM
    density, potential, scaled_all, meta_all, union_all, flip_all = pl.pallas_call(
        functools.partial(region_kernel, n, regions),
        out_shape=(
            S((8, here), f32),
            S((8, here), f32),
            S((n, 8, here), f32),
            S((n, 8, TB), i32),
            S((n, here, wide), bf16),
            S((n, wide, here), bf16),
        ),
        in_specs=[ANY, VM, VM, VM, ANY, SM, SM, SM],
        out_specs=(VM, VM, VM, ANY, ANY, ANY),
        scratch_shapes=[
            V((2, KM, here), bf16),
            V((2, here, KM), bf16),
            V((2, rows, HALF), f32),
            V((rows, here), f32),
            V((rows, HALF), f32),
            V((n * stored, TB, TB), bf16),
            V((wide, wide), bf16),
            V((2, here, wide), bf16),
            V((2, wide, here), bf16),
            V((n, 8, here), f32),
            V((n, 8, here), f32),
            V((rows, KM), f32),
            V((n, rows, KM), f32),
            V((8, KM), f32),
            V((regions, 8, KM), f32),
            V((8, here), f32),
            pltpu.SMEM((n, 8, TB), i32),
            dma((batches, blocks)),
            dma((2,)),
            dma((batches, n)), dma((batches, n)),
            dma((n,)), dma((n,)), dma((n,)), dma((n,)), dma((n,)), dma((n,)),
            dma((regions,)), dma((regions,)), dma((n,)), dma((n,)), dma((n,)), dma((n,)),
            *[V((batches, blocks + 1, points, TB), bf16) for _ in range(n)],
        ],
        compiler_params=pltpu.CompilerParams(collective_id=0, has_side_effects=True),
        name="region",
    )(
        orbitals, meta, point_coords, point_weights.reshape(1, here), dens_tiles,
        batch_atoms, batch_weights, atom_grid_index,
    )
    ham_tiles, density, potential = pl.pallas_call(
        hamilton_kernel,
        grid=(n,),
        out_shape=(
            S((stored, TB, TB), bf16), S((here // TB, TB), f32), S((here // TB, TB), f32),
        ),
        in_specs=[
            SM,
            pl.BlockSpec((1, here, wide), lambda e: (e, 0, 0)),
            pl.BlockSpec((1, wide, here), lambda e: (e, 0, 0)),
            pl.BlockSpec((1, 8, here), lambda e: (e, 0, 0)),
            VM,
            VM,
        ],
        out_specs=(VM, VM, VM),
        scratch_shapes=[
            V((stored, TB, TB), f32),
            V((here, wide), bf16),
            V((union, wide, TB), f32),
            pltpu.SMEM((listed + 1,), i32),
        ],
        name="hamilton",
    )(meta_all, union_all, flip_all, scaled_all, density, potential)
    return density.reshape(-1), potential.reshape(-1), ham_tiles


def solution(mesh):
    body = functools.partial(on_device, mesh.shape["dev"], mesh.shape["grp"])
    in_specs = (
        P(("grp", "dev"), None, None),
        P(("grp", "dev"), None, None),
        P(None, ("grp", "dev")),
        P(("grp", "dev")),
        P(("grp", "dev"), None),
        P(("grp", "dev"), None),
        P(("grp", "dev")),
        P(("grp", "dev"), None),
        P(("grp", "dev"), None),
        P(None, "grp"),
    )
    out_specs = (P(("grp", "dev")), P(("grp", "dev")), P(("grp", "dev"), None, None))
    return jax.shard_map(body, mesh=mesh, in_specs=in_specs, out_specs=out_specs, check_vma=False)
```
